32 devices in a mesh: dp: 16 (over z, y, x), mp: 2 (over core).
Axes of the slice: x: 2, y: 2, z: 4, core: 2. Of those that a mesh axis runs over, the one named last changes fastest.
Arguments:
- tokens: bfloat16 [512, 7168], P('dp', 'mp'), may hold values from -6 to 6
- gate_weight: bfloat16 [7168, 18432], P('mp', 'dp'), may hold values from -0.0625 to 0.0625
- up_weight: bfloat16 [7168, 18432], P('mp', 'dp'), may hold values from -0.0625 to 0.0625
- down_weight: bfloat16 [18432, 7168], P('dp', 'mp'), may hold values from -0.046875 to 0.046875
- gate_round: bfloat16 [7168, 18432], P('mp', 'dp'), may hold values from -8 to 8
- up_round: bfloat16 [7168, 18432], P('mp', 'dp'), may hold values from -8 to 8
- down_round: bfloat16 [18432, 7168], P('dp', 'mp'), may hold values from -8 to 8
- quant_scale: float32 [2, 18432], P(None, 'dp'), may hold values from 0.3 to 3
- quant_bits: int32 [2, 18432], P(None, 'dp'), may hold values from 2 to 4
- quant_zero: int32 [2, 18432], P(None, 'dp'), may hold values from 0 to 2
- down_scale: float32 [7168], P('mp'), may hold values from 0.3 to 3
- down_bits: int32 [7168], P('mp'), may hold values from 2 to 4
- down_zero: int32 [7168], P('mp'), may hold values from 0 to 2
- fisher: float32 [512], replicated, may hold values from 1 to 300, as said below
Outputs:
- loss_value: float32 [], replicated
- grad_gate: bfloat16 [7168, 18432], P('mp', 'dp')
- grad_up: bfloat16 [7168, 18432], P('mp', 'dp')
- grad_down: bfloat16 [18432, 7168], P('dp', 'mp')
The draws below stay inside these ranges and needn't reach their ends.
Inputs may be any that keep to these rules, and one draw needn't show every extreme that they name: `fisher`: positive weights.
All inputs are finite; a program needn't handle non-finite values.
Results may differ from the reference program's by a relative error of at most 0.0059.
Values may be sent and summed in bfloat16 or wider, within the bound.
A program may use at most 192 MiB of HBM per device.

```python
import math
import jax
import jax.numpy as jnp

D = 7168
FF = 18432
TOKENS = 512


def draw_fisher(key, part):
    position = jnp.arange(TOKENS, dtype=jnp.float32) / max(TOKENS - 1, 1)
    growth = math.log(3.0)
    spread = math.log(10.0)
    jitter = jax.random.uniform(key, (TOKENS,), jnp.float32, 0.0, spread)
    return jnp.exp(growth * position + jitter).astype(jnp.float32)


def set_ends(entries, stream_key, smallest, top_value):
    extent = entries.shape
    place = [jax.random.randint(jax.random.fold_in(stream_key, axis), (), 0, extent[axis]) for axis in range(len(extent))]
    entries = entries.at[tuple(place)].set(smallest)
    longest = extent.index(max(extent))
    place[longest] = (place[longest] + 1) % extent[longest]
    return entries.at[tuple(place)].set(top_value)


def block_scale(rng, shape, pieces, least, top_value):
    def one(axis_at, parts):
        steps = jax.random.uniform(jax.random.fold_in(jax.random.fold_in(rng, 6), axis_at), (parts,), jnp.float32, least / len(pieces), top_value / len(pieces))
        return jnp.repeat(jnp.exp(steps), shape[axis_at] // parts).reshape((-1,) + (1,) * (len(shape) - axis_at - 1))

    level = one(*pieces[0])
    for cut in pieces[1:]:
        level = level * one(*cut)
    return level


def centred(key, dims, deviation, limit, pieces=(), kind=jnp.bfloat16):
    gain = block_scale(key, dims, pieces, -0.22, 0.18) if pieces else 1.0
    values = jax.random.normal(key, dims, jnp.float32) * deviation * gain
    return jnp.minimum(jnp.maximum(values, -limit), limit).astype(kind)


def setup_inputs(seed: int = 0) -> dict:
    key_of = jax.random.split(jax.random.key(seed), 15)
    return {
        "tokens": centred(key_of[0], (TOKENS, D), 1.0, 6.0, ((0, 16), (1, 2))),
        "gate_weight": centred(key_of[1], (D, FF), D ** -0.5, 0.0625, ((0, 2), (1, 16))),
        "up_weight": centred(key_of[2], (D, FF), D ** -0.5, 0.0625, ((0, 2), (1, 16))),
        "down_weight": centred(key_of[3], (FF, D), FF ** -0.5, 0.046875, ((0, 16), (1, 2))),
        "gate_round": centred(key_of[4], (D, FF), 2.0, 8.0, ((0, 2), (1, 16))),
        "up_round": centred(key_of[5], (D, FF), 2.0, 8.0, ((0, 2), (1, 16))),
        "down_round": centred(key_of[6], (FF, D), 2.0, 8.0, ((0, 16), (1, 2))),
        "quant_scale": jnp.clip(jnp.exp(math.log(3.0) - 2.3025851 * jax.random.uniform(key_of[7], (2, FF), jnp.float32) ** block_scale(key_of[7], (2, FF), ((1, 16),), -0.2, 0.2)), 0.3, 3.0),
        "quant_bits": set_ends(jax.random.randint(key_of[8], (2, FF), 2, 5), jax.random.fold_in(key_of[8], 1), 2, 4).astype(jnp.int32),
        "quant_zero": set_ends(jax.random.randint(key_of[9], (2, FF), 0, 3), jax.random.fold_in(key_of[9], 1), 0, 2).astype(jnp.int32),
        "down_scale": jnp.clip(jnp.exp(math.log(3.0) - 2.3025851 * jax.random.uniform(key_of[10], (D,), jnp.float32) ** block_scale(key_of[10], (D,), ((0, 2),), -0.2, 0.2)), 0.3, 3.0),
        "down_bits": set_ends(jax.random.randint(key_of[11], (D,), 2, 5), jax.random.fold_in(key_of[11], 1), 2, 4).astype(jnp.int32),
        "down_zero": set_ends(jax.random.randint(key_of[12], (D,), 0, 3), jax.random.fold_in(key_of[12], 1), 0, 2).astype(jnp.int32),
        "fisher": draw_fisher(jax.random.fold_in(key_of[14], 71), 0),
    }


def soft_weight(weight, variable, channel_scale, bit_width, zero_point, fan_in):
    quant_step = channel_scale / jnp.sqrt(jnp.float32(fan_in))
    offset = jnp.clip(1.2 * jax.nn.sigmoid(variable.astype(jnp.float32)) - 0.1, 0.0, 1.0)
    ceiling = (jnp.left_shift(jnp.int32(1), bit_width) - 1).astype(jnp.float32)
    zero_level = zero_point.astype(jnp.float32)
    levels = jnp.clip(weight.astype(jnp.float32) / quant_step + offset - 0.5 + zero_level, 0.0, ceiling)
    return (quant_step * (levels - zero_level)).astype(jnp.bfloat16)

def reference(tokens, gate_weight, up_weight, down_weight, gate_round, up_round, down_round, quant_scale, quant_bits, quant_zero, down_scale, down_bits, down_zero, fisher):
    gate_student = soft_weight(gate_weight, gate_round, quant_scale[0], quant_bits[0], quant_zero[0], D)
    up_student = soft_weight(up_weight, up_round, quant_scale[1], quant_bits[1], quant_zero[1], D)
    down_student = soft_weight(down_weight, down_round, down_scale, down_bits, down_zero, FF)
    gate_teacher = jnp.dot(tokens, gate_weight, preferred_element_type=jnp.float32)
    up_teacher = jnp.dot(tokens, up_weight, preferred_element_type=jnp.float32)
    gate_own = jnp.dot(tokens, gate_student, preferred_element_type=jnp.float32)
    up_own = jnp.dot(tokens, up_student, preferred_element_type=jnp.float32)
    hidden_teacher = (jax.nn.silu(gate_teacher) * up_teacher).astype(jnp.bfloat16)
    hidden_student = (jax.nn.silu(gate_own) * up_own).astype(jnp.bfloat16)
    output_student = jnp.dot(hidden_student, down_student, preferred_element_type=jnp.float32)
    output_teacher = jnp.dot(hidden_teacher, down_weight, preferred_element_type=jnp.float32)
    residual = output_student - output_teacher
    weighted = fisher[:, None] * residual
    loss_value = jnp.sum(weighted * residual) / (TOKENS * D)
    out_grad = (2.0 * weighted).astype(jnp.bfloat16)
    grad_down = jnp.dot(hidden_student.T, out_grad, preferred_element_type=jnp.float32).astype(jnp.bfloat16)
    hidden_grad = jnp.dot(out_grad, down_student.T, preferred_element_type=jnp.float32)
    sigmoid_gate = jax.nn.sigmoid(gate_own)
    gate_grad = (hidden_grad * up_own * sigmoid_gate * (1.0 + gate_own * (1.0 - sigmoid_gate))).astype(jnp.bfloat16)
    up_grad = (hidden_grad * gate_own * sigmoid_gate).astype(jnp.bfloat16)
    grad_gate = jnp.dot(tokens.T, gate_grad, preferred_element_type=jnp.float32).astype(jnp.bfloat16)
    grad_up = jnp.dot(tokens.T, up_grad, preferred_element_type=jnp.float32).astype(jnp.bfloat16)
    return (loss_value, grad_gate, grad_up, grad_down)
```

```python
import functools

import jax
import jax.numpy as jnp
from jax import lax
from jax.experimental import pallas as pl
from jax.experimental.pallas import tpu as pltpu
from jax.sharding import PartitionSpec as P

D = 7168
FF = 18432
MESH = pl.DeviceIdType.MESH
LANES = 128


def ring_index(position, count):
    if count % 4:
        return position
    depth = count // 4
    column, run = position // depth, position % depth
    level = run + (column % 2) * (depth - 1 - 2 * run)
    return level * 4 + column + (column // 2) * (5 - 2 * column)


def ring_position(index, count):
    if count % 4:
        return index
    depth = count // 4
    level, corner = index // 4, index % 4
    column = corner + (corner // 2) * (5 - 2 * corner)
    return column * depth + level + (column % 2) * (depth - 1 - 2 * level)


def column_pieces(columns, parts=4):
    tiles = columns // LANES
    edges = [tiles * k // parts * LANES for k in range(parts)] + [columns]
    return [(lo, hi) for lo, hi in zip(edges[:-1], edges[1:]) if hi > lo]


def exchange_kernel(
    count,
    peers,
    terms_ref,
    scale_ref,
    grad_ref,
    loss_ref,
    slots,
    loss_peer,
    loss_ring,
    rs_send,
    rs_recv,
    ag_send,
    ag_recv,
    lp_send,
    lp_recv,
    lr_send,
    lr_recv,
):
    me = lax.axis_index("dp")
    lane = lax.axis_index("mp")
    place = ring_position(me, count)
    right = ring_index((place + 1) % count, count)
    left = ring_index((place + count - 1) % count, count)
    rows, columns = slots.shape[1], slots.shape[2]
    pieces = column_pieces(columns)
    steps = count - 1

    barrier = pltpu.get_barrier_semaphore()
    for other in (left, right):
        pl.semaphore_signal(barrier, inc=1, device_id={"dp": other}, device_id_type=MESH)
    for j in range(1, peers):
        pl.semaphore_signal(
            barrier, inc=1, device_id={"mp": (lane + j) % peers}, device_id_type=MESH
        )
    pl.semaphore_wait(barrier, 2 + peers - 1)

    def block_rows(position):
        start = ring_index((position + 2 * count) % count, count) * rows
        return pl.ds(pl.multiple_of(start, rows), rows)

    def target(k):
        return {"dp": right if k % 2 == 0 else left}

    def sign(k):
        return 1 if k % 2 == 0 else -1

    def reduce_copy(k, step, source):
        lo, hi = pieces[k]
        return pltpu.make_async_remote_copy(
            src_ref=source,
            dst_ref=slots.at[step, :, lo:hi],
            send_sem=rs_send.at[step, k],
            recv_sem=rs_recv.at[step, k],
            device_id=target(k),
            device_id_type=MESH,
        )

    def gather_copy(k, step):
        lo, hi = pieces[k]
        part = grad_ref.at[block_rows(place - sign(k) * step), lo:hi]
        return pltpu.make_async_remote_copy(
            src_ref=part,
            dst_ref=part,
            send_sem=ag_send.at[step, k],
            recv_sem=ag_recv.at[step, k],
            device_id=target(k),
            device_id_type=MESH,
        )

    def gather_arrival(k, step):
        lo, hi = pieces[k]
        part = grad_ref.at[block_rows(place - sign(k) * (step + 1)), lo:hi]
        return pltpu.make_async_remote_copy(
            src_ref=part,
            dst_ref=part,
            send_sem=ag_send.at[step, k],
            recv_sem=ag_recv.at[step, k],
            device_id=target(k),
            device_id_type=MESH,
        )

    def loss_copy(step, slot):
        return pltpu.make_async_remote_copy(
            src_ref=loss_ring.at[slot],
            dst_ref=loss_ring.at[step + 1],
            send_sem=lr_send.at[step],
            recv_sem=lr_recv.at[step],
            device_id={"dp": right},
            device_id_type=MESH,
        )

    for k, (lo, hi) in enumerate(pieces):
        reduce_copy(k, 0, terms_ref.at[block_rows(place - sign(k)), lo:hi]).start()

    def reduce_step(step, carry):
        for k, (lo, hi) in enumerate(pieces):
            landed = slots.at[step, :, lo:hi]
            reduce_copy(k, step, landed).wait_recv()
            own = terms_ref[block_rows(place - sign(k) * (step + 2)), lo:hi]
            slots[step, :, lo:hi] = (
                slots[step, :, lo:hi].astype(jnp.float32) + own.astype(jnp.float32)
            ).astype(jnp.bfloat16)
            reduce_copy(k, step + 1, landed).start()
        return carry

    lax.fori_loop(0, steps - 1, reduce_step, 0)

    scale = scale_ref[...]
    total = jnp.zeros((rows, LANES), jnp.float32)
    for k, (lo, hi) in enumerate(pieces):
        last = slots.at[steps - 1, :, lo:hi]
        reduce_copy(k, steps - 1, last).wait_recv()
        summed = slots[steps - 1, :, lo:hi].astype(jnp.float32) + terms_ref[
            block_rows(place), lo:hi
        ].astype(jnp.float32)
        weighted = scale * summed
        grad_ref[block_rows(place), lo:hi] = (2.0 * weighted).astype(jnp.bfloat16)
        gather_copy(k, 0).start()
        squares = weighted * summed
        for at in range(0, hi - lo, LANES):
            total = total + squares[:, at : at + LANES]

    folded = total[:8]
    for at in range(8, rows, 8):
        folded = folded + total[at : at + 8]
    loss_peer[0] = folded

    def peer_copy(j):
        return pltpu.make_async_remote_copy(
            src_ref=loss_peer.at[0],
            dst_ref=loss_peer.at[j],
            send_sem=lp_send.at[j - 1],
            recv_sem=lp_recv.at[j - 1],
            device_id={"mp": (lane + j) % peers},
            device_id_type=MESH,
        )

    for j in range(1, peers):
        peer_copy(j).start()
    for j in range(1, peers):
        peer_copy(j).wait_recv()
        folded = folded + loss_peer[j]
    loss_ring[0] = folded
    loss_copy(0, 0).start()

    def gather_step(step, carry):
        for k in range(len(pieces)):
            gather_arrival(k, step).wait_recv()
            gather_copy(k, step + 1).start()
        loss_copy(step, step).wait_recv()
        loss_copy(step + 1, step + 1).start()
        return carry

    lax.fori_loop(0, steps - 1, gather_step, 0)
    for k in range(len(pieces)):
        gather_arrival(k, steps - 1).wait_recv()
    loss_copy(steps - 1, steps - 1).wait_recv()
    loss_ref[...] = jnp.sum(loss_ring[...], axis=0)

    def drain(step, carry):
        for k, (lo, hi) in enumerate(pieces):
            reduce_copy(k, step, slots.at[step, :, lo:hi]).wait_send()
            gather_copy(k, step).wait_send()
        loss_copy(step, step).wait_send()
        return carry

    lax.fori_loop(0, steps, drain, 0)
    for j in range(1, peers):
        peer_copy(j).wait_send()


def exchange(terms, token_weight, count, peers):
    rows, columns = terms.shape[0] // count, terms.shape[1]
    steps, parts = count - 1, len(column_pieces(columns))
    spec = pl.BlockSpec(memory_space=pltpu.VMEM)
    dma = pltpu.SemaphoreType.DMA
    grad, loss = pl.pallas_call(
        functools.partial(exchange_kernel, count, peers),
        out_shape=(
            jax.ShapeDtypeStruct(terms.shape, jnp.bfloat16),
            jax.ShapeDtypeStruct((8, LANES), jnp.float32),
        ),
        in_specs=[spec, spec],
        out_specs=(spec, spec),
        scratch_shapes=[
            pltpu.VMEM((steps, rows, columns), jnp.bfloat16),
            pltpu.VMEM((peers, 8, LANES), jnp.float32),
            pltpu.VMEM((count, 8, LANES), jnp.float32),
            dma((steps, parts)),
            dma((steps, parts)),
            dma((steps, parts)),
            dma((steps, parts)),
            dma((peers - 1,)),
            dma((peers - 1,)),
            dma((steps,)),
            dma((steps,)),
        ],
        compiler_params=pltpu.CompilerParams(collective_id=0, has_side_effects=True),
    )(terms, token_weight)
    return grad, jnp.sum(loss)


def soft_weight(weight, variable, channel_scale, bit_width, zero_point, fan_in):
    quant_step = channel_scale / jnp.sqrt(jnp.float32(fan_in))
    offset = jnp.clip(1.2 * jax.nn.sigmoid(variable.astype(jnp.float32)) - 0.1, 0.0, 1.0)
    ceiling = (jnp.left_shift(jnp.int32(1), bit_width) - 1).astype(jnp.float32)
    zero_level = zero_point.astype(jnp.float32)
    levels = jnp.clip(
        weight.astype(jnp.float32) / quant_step + offset - 0.5 + zero_level, 0.0, ceiling
    )
    return (quant_step * (levels - zero_level)).astype(jnp.bfloat16)


def contract_rows(left, right):
    return lax.dot_general(
        left, right, (((0,), (0,)), ((), ())), preferred_element_type=jnp.float32
    )


def shards(
    count,
    peers,
    tokens,
    gate_weight,
    up_weight,
    down_weight,
    gate_round,
    up_round,
    down_round,
    quant_scale,
    quant_bits,
    quant_zero,
    down_scale,
    down_bits,
    down_zero,
    fisher,
):
    own_rows = tokens.shape[0]
    hidden_cols = gate_weight.shape[1]
    all_tokens = lax.all_gather(tokens, "dp", axis=0, tiled=True)
    total_rows = all_tokens.shape[0]
    gate_student = soft_weight(
        gate_weight, gate_round, quant_scale[0], quant_bits[0], quant_zero[0], D
    )
    up_student = soft_weight(up_weight, up_round, quant_scale[1], quant_bits[1], quant_zero[1], D)
    stacked = jnp.concatenate([gate_weight, up_weight, gate_student, up_student], axis=1)
    partial_value = jnp.dot(all_tokens, stacked, preferred_element_type=jnp.float32)
    shares = lax.psum_scatter(partial_value, "mp", scatter_dimension=0, tiled=True)
    gate_teacher = shares[:, :hidden_cols]
    up_teacher = shares[:, hidden_cols : 2 * hidden_cols]
    gate_own = shares[:, 2 * hidden_cols : 3 * hidden_cols]
    up_own = shares[:, 3 * hidden_cols :]
    hidden_teacher = (jax.nn.silu(gate_teacher) * up_teacher).astype(jnp.bfloat16)
    hidden_student = (jax.nn.silu(gate_own) * up_own).astype(jnp.bfloat16)
    hidden = lax.all_gather(
        jnp.concatenate([hidden_teacher, hidden_student], axis=1), "mp", axis=0, tiled=True
    )
    down_student = soft_weight(down_weight, down_round, down_scale, down_bits, down_zero, FF)
    terms = jnp.dot(
        hidden[:, hidden_cols:], down_student, preferred_element_type=jnp.float32
    ) - jnp.dot(hidden[:, :hidden_cols], down_weight, preferred_element_type=jnp.float32)
    token_weight = lax.dynamic_slice_in_dim(fisher, lax.axis_index("dp") * own_rows, own_rows)
    out_grad, loss_sum = exchange(
        terms.astype(jnp.bfloat16), token_weight[:, None], count, peers
    )
    loss_value = loss_sum / (total_rows * D)
    grad_down = contract_rows(hidden[:, hidden_cols:], out_grad).astype(jnp.bfloat16)
    hidden_part = lax.dot_general(
        out_grad, down_student, (((1,), (1,)), ((), ())), preferred_element_type=jnp.float32
    )
    hidden_grad = lax.psum_scatter(hidden_part, "mp", scatter_dimension=0, tiled=True)
    sigmoid_gate = jax.nn.sigmoid(gate_own)
    gate_grad = (
        hidden_grad * up_own * sigmoid_gate * (1.0 + gate_own * (1.0 - sigmoid_gate))
    ).astype(jnp.bfloat16)
    up_grad = (hidden_grad * gate_own * sigmoid_gate).astype(jnp.bfloat16)
    both_grads = lax.all_gather(
        jnp.concatenate([gate_grad, up_grad], axis=1), "mp", axis=0, tiled=True
    )
    grad_gate = contract_rows(all_tokens, both_grads[:, :hidden_cols]).astype(jnp.bfloat16)
    grad_up = contract_rows(all_tokens, both_grads[:, hidden_cols:]).astype(jnp.bfloat16)
    return (loss_value, grad_gate, grad_up, grad_down)


def solution(mesh):
    in_specs = (
        P("dp", "mp"),
        P("mp", "dp"),
        P("mp", "dp"),
        P("dp", "mp"),
        P("mp", "dp"),
        P("mp", "dp"),
        P("dp", "mp"),
        P(None, "dp"),
        P(None, "dp"),
        P(None, "dp"),
        P("mp"),
        P("mp"),
        P("mp"),
        P(),
    )
    out_specs = (P(), P("mp", "dp"), P("mp", "dp"), P("dp", "mp"))
    body = functools.partial(shards, mesh.shape["dp"], mesh.shape["mp"])
    return jax.shard_map(body, mesh=mesh, in_specs=in_specs, out_specs=out_specs, check_vma=False)
```

```python
import functools

import jax
import jax.numpy as jnp
from jax import lax
from jax.experimental import pallas as pl
from jax.experimental.layout import Layout, with_layout_constraint
from jax.experimental.pallas import tpu as pltpu
from jax.sharding import PartitionSpec as P

D = 7168
FF = 18432
MESH = pl.DeviceIdType.MESH
LANES = 128


def ring_index(position, count):
    if count % 4:
        return position
    depth = count // 4
    column, run = position // depth, position % depth
    level = run + (column % 2) * (depth - 1 - 2 * run)
    return level * 4 + column + (column // 2) * (5 - 2 * column)


def ring_position(index, count):
    if count % 4:
        return index
    depth = count // 4
    level, corner = index // 4, index % 4
    column = corner + (corner // 2) * (5 - 2 * corner)
    return column * depth + level + (column % 2) * (depth - 1 - 2 * level)


def column_pieces(columns, parts=8):
    tiles = columns // LANES
    edges = [tiles * k // parts * LANES for k in range(parts)] + [columns]
    return [(lo, hi) for lo, hi in zip(edges[:-1], edges[1:]) if hi > lo]


def exchange_kernel(
    count,
    peers,
    terms_ref,
    scale_ref,
    grad_ref,
    loss_ref,
    slots,
    loss_peer,
    loss_ring,
    rs_send,
    rs_recv,
    ag_send,
    ag_recv,
    lp_send,
    lp_recv,
    lr_send,
    lr_recv,
):
    me = lax.axis_index("dp")
    lane = lax.axis_index("mp")
    place = ring_position(me, count)
    right = ring_index((place + 1) % count, count)
    left = ring_index((place + count - 1) % count, count)
    rows, columns = slots.shape[1], slots.shape[2]
    pieces = column_pieces(columns)
    steps = count - 1

    barrier = pltpu.get_barrier_semaphore()
    for other in (left, right):
        pl.semaphore_signal(barrier, inc=1, device_id={"dp": other}, device_id_type=MESH)
    for j in range(1, peers):
        pl.semaphore_signal(
            barrier, inc=1, device_id={"mp": (lane + j) % peers}, device_id_type=MESH
        )
    pl.semaphore_wait(barrier, 2 + peers - 1)

    def block_rows(position):
        start = ring_index((position + 2 * count) % count, count) * rows
        return pl.ds(pl.multiple_of(start, rows), rows)

    turn = 1 - 2 * (lane % 2)
    onward = ring_index((place + turn + count) % count, count)

    def target(k):
        return {"dp": onward}

    def sign(k):
        return turn

    def reduce_copy(k, step, source):
        lo, hi = pieces[k]
        return pltpu.make_async_remote_copy(
            src_ref=source,
            dst_ref=slots.at[step, :, lo:hi],
            send_sem=rs_send.at[step, k],
            recv_sem=rs_recv.at[step, k],
            device_id=target(k),
            device_id_type=MESH,
        )

    def gather_copy(k, step):
        lo, hi = pieces[k]
        part = grad_ref.at[block_rows(place - sign(k) * step), lo:hi]
        return pltpu.make_async_remote_copy(
            src_ref=part,
            dst_ref=part,
            send_sem=ag_send.at[step, k],
            recv_sem=ag_recv.at[step, k],
            device_id=target(k),
            device_id_type=MESH,
        )

    def gather_arrival(k, step):
        lo, hi = pieces[k]
        part = grad_ref.at[block_rows(place - sign(k) * (step + 1)), lo:hi]
        return pltpu.make_async_remote_copy(
            src_ref=part,
            dst_ref=part,
            send_sem=ag_send.at[step, k],
            recv_sem=ag_recv.at[step, k],
            device_id=target(k),
            device_id_type=MESH,
        )

    def loss_copy(step, slot):
        return pltpu.make_async_remote_copy(
            src_ref=loss_ring.at[slot],
            dst_ref=loss_ring.at[step + 1],
            send_sem=lr_send.at[step],
            recv_sem=lr_recv.at[step],
            device_id={"dp": onward},
            device_id_type=MESH,
        )

    for k, (lo, hi) in enumerate(pieces):
        reduce_copy(k, 0, terms_ref.at[block_rows(place - sign(k)), lo:hi]).start()

    def reduce_step(step, carry):
        for k, (lo, hi) in enumerate(pieces):
            landed = slots.at[step, :, lo:hi]
            reduce_copy(k, step, landed).wait_recv()
            own = terms_ref[block_rows(place - sign(k) * (step + 2)), lo:hi]
            slots[step, :, lo:hi] = (
                slots[step, :, lo:hi].astype(jnp.float32) + own.astype(jnp.float32)
            ).astype(jnp.bfloat16)
            reduce_copy(k, step + 1, landed).start()
        return carry

    lax.fori_loop(0, steps - 1, reduce_step, 0)

    scale = scale_ref[...]
    total = jnp.zeros((rows, LANES), jnp.float32)
    for k, (lo, hi) in enumerate(pieces):
        last = slots.at[steps - 1, :, lo:hi]
        reduce_copy(k, steps - 1, last).wait_recv()
        summed = slots[steps - 1, :, lo:hi].astype(jnp.float32) + terms_ref[
            block_rows(place), lo:hi
        ].astype(jnp.float32)
        weighted = scale * summed
        grad_ref[block_rows(place), lo:hi] = (2.0 * weighted).astype(jnp.bfloat16)
        gather_copy(k, 0).start()
        squares = weighted * summed
        for at in range(0, hi - lo, LANES):
            total = total + squares[:, at : at + LANES]

    folded = total[:8]
    for at in range(8, rows, 8):
        folded = folded + total[at : at + 8]
    loss_peer[0] = folded

    def peer_copy(j):
        return pltpu.make_async_remote_copy(
            src_ref=loss_peer.at[0],
            dst_ref=loss_peer.at[j],
            send_sem=lp_send.at[j - 1],
            recv_sem=lp_recv.at[j - 1],
            device_id={"mp": (lane + j) % peers},
            device_id_type=MESH,
        )

    for j in range(1, peers):
        peer_copy(j).start()
    for j in range(1, peers):
        peer_copy(j).wait_recv()
        folded = folded + loss_peer[j]
    loss_ring[0] = folded
    loss_copy(0, 0).start()

    def gather_step(step, carry):
        for k in range(len(pieces)):
            gather_arrival(k, step).wait_recv()
            gather_copy(k, step + 1).start()
        loss_copy(step, step).wait_recv()
        loss_copy(step + 1, step + 1).start()
        return carry

    lax.fori_loop(0, steps - 1, gather_step, 0)
    for k in range(len(pieces)):
        gather_arrival(k, steps - 1).wait_recv()
    loss_copy(steps - 1, steps - 1).wait_recv()
    loss_ref[...] = jnp.sum(loss_ring[...], axis=0)

    def drain(step, carry):
        for k, (lo, hi) in enumerate(pieces):
            reduce_copy(k, step, slots.at[step, :, lo:hi]).wait_send()
            gather_copy(k, step).wait_send()
        loss_copy(step, step).wait_send()
        return carry

    lax.fori_loop(0, steps, drain, 0)
    for j in range(1, peers):
        peer_copy(j).wait_send()


def exchange(terms, token_weight, count, peers):
    rows, columns = terms.shape[0] // count, terms.shape[1]
    steps, parts = count - 1, len(column_pieces(columns))
    spec = pl.BlockSpec(memory_space=pltpu.VMEM)
    dma = pltpu.SemaphoreType.DMA
    grad, loss = pl.pallas_call(
        functools.partial(exchange_kernel, count, peers),
        out_shape=(
            jax.ShapeDtypeStruct(terms.shape, jnp.bfloat16),
            jax.ShapeDtypeStruct((8, LANES), jnp.float32),
        ),
        in_specs=[spec, spec],
        out_specs=(spec, spec),
        scratch_shapes=[
            pltpu.VMEM((steps, rows, columns), jnp.bfloat16),
            pltpu.VMEM((peers, 8, LANES), jnp.float32),
            pltpu.VMEM((count, 8, LANES), jnp.float32),
            dma((steps, parts)),
            dma((steps, parts)),
            dma((steps, parts)),
            dma((steps, parts)),
            dma((peers - 1,)),
            dma((peers - 1,)),
            dma((steps,)),
            dma((steps,)),
        ],
        compiler_params=pltpu.CompilerParams(collective_id=0, has_side_effects=True),
    )(terms, token_weight)
    return grad, jnp.sum(loss)


def gather_kernel(
    count,
    stride,
    tokens_ref,
    channel_ref,
    gate_ref,
    gate_round_ref,
    up_ref,
    up_round_ref,
    gate_out,
    up_out,
    all_ref,
    held,
    send_sem,
    recv_sem,
    local_sem,
):
    at = pl.program_id(0)
    last = pl.num_programs(0) - 1
    me = lax.axis_index("dp")
    place = ring_position(me, count)
    right = ring_index((place + 1) % count, count)
    left = ring_index((place + count - 1) % count, count)
    rows, columns = tokens_ref.shape
    pieces = column_pieces(columns)
    steps = count - 1
    sign = 1 - 2 * (lax.axis_index("mp") % 2)
    onward = ring_index((place + sign + count) % count, count)

    def ring_copy(k, step, hop):
        lo, hi = pieces[k]
        start = ring_index((place - sign * (step + hop) + 2 * count) % count, count) * rows
        part = held.at[pl.ds(pl.multiple_of(start, rows), rows), lo:hi]
        return pltpu.make_async_remote_copy(
            src_ref=part,
            dst_ref=part,
            send_sem=send_sem.at[step, k],
            recv_sem=recv_sem.at[step, k],
            device_id={"dp": onward},
            device_id_type=MESH,
        )

    @pl.when(at == 0)
    def _():
        own = pltpu.make_async_copy(
            tokens_ref, held.at[pl.ds(pl.multiple_of(me * rows, rows), rows), :], local_sem
        )
        own.start()
        barrier = pltpu.get_barrier_semaphore()
        for other in (left, right):
            pl.semaphore_signal(barrier, inc=1, device_id={"dp": other}, device_id_type=MESH)
        pl.semaphore_wait(barrier, 2)
        own.wait()
        for k in range(len(pieces)):
            ring_copy(k, 0, 0).start()

    def relay(step, carry):
        for k in range(len(pieces)):
            ring_copy(k, step, 1).wait_recv()
            ring_copy(k, step + 1, 0).start()
        return carry

    @pl.when((at > 0) & (at % stride == 0) & (at // stride < steps))
    def _():
        relay(at // stride - 1, 0)

    chunk = 16
    tile = gate_ref.shape[0]

    def weights(step, carry):
        here = pl.ds(pl.multiple_of(step * chunk, chunk), chunk)
        for row, weight, rounding, out in (
            (0, gate_ref, gate_round_ref, gate_out),
            (1, up_ref, up_round_ref, up_out),
        ):
            unit, inverse, low, high = (channel_ref[4 * row + j : 4 * row + j + 1] for j in range(4))
            spread = jnp.tanh(0.5 * rounding[here, :].astype(jnp.float32))
            offset = jnp.clip(0.6 * spread, -0.5, 0.5)
            levels = weight[here, :].astype(jnp.float32) * inverse + offset
            levels = jnp.minimum(jnp.maximum(levels, low), high)
            out[here, :] = (unit * levels).astype(jnp.bfloat16)
        return carry

    lax.fori_loop(0, tile // chunk, weights, 0)

    @pl.when(at == last)
    def _():
        reached = jnp.minimum(last // stride, steps - 1)
        lax.fori_loop(reached, steps - 1, relay, 0)
        for k in range(len(pieces)):
            ring_copy(k, steps - 1, 1).wait_recv()
        done = pltpu.make_async_copy(held, all_ref, local_sem)
        done.start()

        def drain(step, carry):
            for k in range(len(pieces)):
                ring_copy(k, step, 0).wait_send()
            return carry

        lax.fori_loop(0, steps, drain, 0)
        done.wait()


def gather_and_round(tokens, weights, rounds, scale, bits, zero, count):
    rows, columns = tokens.shape
    depth, width = weights[0].shape
    steps, parts = count - 1, len(column_pieces(columns))
    tiles = max(g for g in range(1, 33) if depth % (16 * g) == 0)
    tile = depth // tiles
    root = jnp.sqrt(jnp.float32(D))
    unit = scale / root
    zero_level = zero.astype(jnp.float32)
    ceiling = (jnp.left_shift(jnp.int32(1), bits) - 1).astype(jnp.float32)
    channel = jnp.stack([unit, 1.0 / unit, -zero_level, ceiling - zero_level], axis=1)
    channel = channel.reshape(8, width)
    block = pl.BlockSpec((tile, width), lambda i: (i, 0))
    anywhere = pl.BlockSpec(memory_space=pl.ANY)
    dma = pltpu.SemaphoreType.DMA
    return pl.pallas_call(
        functools.partial(gather_kernel, count, max(1, tiles // count)),
        grid=(tiles,),
        out_shape=(
            jax.ShapeDtypeStruct((depth, width), jnp.bfloat16),
            jax.ShapeDtypeStruct((depth, width), jnp.bfloat16),
            jax.ShapeDtypeStruct((count * rows, columns), jnp.bfloat16),
        ),
        in_specs=[anywhere, pl.BlockSpec((8, width), lambda i: (0, 0))] + [block] * 4,
        out_specs=(block, block, anywhere),
        scratch_shapes=[
            pltpu.VMEM((count * rows, columns), jnp.bfloat16),
            dma((steps, parts)),
            dma((steps, parts)),
            dma(()),
        ],
        compiler_params=pltpu.CompilerParams(
            collective_id=1, has_side_effects=True, dimension_semantics=("arbitrary",)
        ),
    )(tokens, channel, weights[0], rounds[0], weights[1], rounds[1])


def soft_weight(weight, variable, channel_scale, bit_width, zero_point, fan_in):
    quant_step = channel_scale / jnp.sqrt(jnp.float32(fan_in))
    offset = jnp.clip(1.2 * jax.nn.sigmoid(variable.astype(jnp.float32)) - 0.1, 0.0, 1.0)
    ceiling = (jnp.left_shift(jnp.int32(1), bit_width) - 1).astype(jnp.float32)
    zero_level = zero_point.astype(jnp.float32)
    levels = jnp.clip(
        weight.astype(jnp.float32) / quant_step + offset - 0.5 + zero_level, 0.0, ceiling
    )
    return (quant_step * (levels - zero_level)).astype(jnp.bfloat16)


def contract_rows(left, right):
    return lax.dot_general(
        left, right, (((0,), (0,)), ((), ())), preferred_element_type=jnp.float32
    )


def shards(
    count,
    peers,
    tokens,
    gate_weight,
    up_weight,
    down_weight,
    gate_round,
    up_round,
    down_round,
    quant_scale,
    quant_bits,
    quant_zero,
    down_scale,
    down_bits,
    down_zero,
    fisher,
):
    own_rows = tokens.shape[0]
    hidden_cols = gate_weight.shape[1]
    gate_student, up_student, all_tokens = gather_and_round(
        tokens,
        (gate_weight, up_weight),
        (gate_round, up_round),
        quant_scale,
        quant_bits,
        quant_zero,
        count,
    )
    total_rows = all_tokens.shape[0]

    stacked = jnp.concatenate([gate_weight, up_weight, gate_student, up_student], axis=1)
    partial_value = jnp.dot(all_tokens, stacked, preferred_element_type=jnp.float32)
    shares = lax.psum_scatter(partial_value, "mp", scatter_dimension=0, tiled=True)
    gate_teacher = shares[:, :hidden_cols]
    up_teacher = shares[:, hidden_cols : 2 * hidden_cols]
    gate_own = shares[:, 2 * hidden_cols : 3 * hidden_cols]
    up_own = shares[:, 3 * hidden_cols :]
    hidden_teacher = (jax.nn.silu(gate_teacher) * up_teacher).astype(jnp.bfloat16)
    hidden_student = (jax.nn.silu(gate_own) * up_own).astype(jnp.bfloat16)
    hidden = lax.all_gather(
        jnp.concatenate([hidden_teacher, hidden_student], axis=1), "mp", axis=0, tiled=True
    )
    down_student = soft_weight(down_weight, down_round, down_scale, down_bits, down_zero, FF)
    terms = jnp.dot(
        hidden[:, hidden_cols:], down_student, preferred_element_type=jnp.float32
    ) - jnp.dot(hidden[:, :hidden_cols], down_weight, preferred_element_type=jnp.float32)
    token_weight = lax.dynamic_slice_in_dim(fisher, lax.axis_index("dp") * own_rows, own_rows)
    out_grad, loss_sum = exchange(
        terms.astype(jnp.bfloat16), token_weight[:, None], count, peers
    )
    loss_value = loss_sum / (total_rows * D)
    grad_down = contract_rows(hidden[:, hidden_cols:], out_grad).astype(jnp.bfloat16)
    hidden_part = lax.dot_general(
        out_grad, down_student, (((1,), (1,)), ((), ())), preferred_element_type=jnp.float32
    )
    hidden_grad = lax.psum_scatter(
        hidden_part.astype(jnp.bfloat16), "mp", scatter_dimension=0, tiled=True
    ).astype(jnp.float32)
    sigmoid_gate = jax.nn.sigmoid(gate_own)
    gate_grad = (
        hidden_grad * up_own * sigmoid_gate * (1.0 + gate_own * (1.0 - sigmoid_gate))
    ).astype(jnp.bfloat16)
    up_grad = (hidden_grad * gate_own * sigmoid_gate).astype(jnp.bfloat16)
    both_grads = lax.all_gather(
        jnp.concatenate([gate_grad, up_grad], axis=1), "mp", axis=0, tiled=True
    )
    grad_gate = contract_rows(all_tokens, both_grads[:, :hidden_cols]).astype(jnp.bfloat16)
    grad_up = contract_rows(all_tokens, both_grads[:, hidden_cols:]).astype(jnp.bfloat16)
    grad_gate = with_layout_constraint(grad_gate, Layout((0, 1)))
    grad_up = with_layout_constraint(grad_up, Layout((0, 1)))
    return (loss_value, grad_gate, grad_up, grad_down)


def solution(mesh):
    in_specs = (
        P("dp", "mp"),
        P("mp", "dp"),
        P("mp", "dp"),
        P("dp", "mp"),
        P("mp", "dp"),
        P("mp", "dp"),
        P("dp", "mp"),
        P(None, "dp"),
        P(None, "dp"),
        P(None, "dp"),
        P("mp"),
        P("mp"),
        P("mp"),
        P(),
    )
    out_specs = (P(), P("mp", "dp"), P("mp", "dp"), P("dp", "mp"))
    body = functools.partial(shards, mesh.shape["dp"], mesh.shape["mp"])
    return jax.shard_map(body, mesh=mesh, in_specs=in_specs, out_specs=out_specs, check_vma=False)
```
